256 devices in a mesh: own: 16 (over x_hi, y, core), rep: 16 (over z, x_lo).
Axes of the slice: x: 4 (x_hi: 2, x_lo: 2; x = x_hi * 2 + x_lo), y: 4, z: 8, core: 2. Of those that a mesh axis runs over, the one named last changes fastest.
Arguments:
- latents: bfloat16 [512, 32, 32, 320], P(('own', 'rep')), may hold values from -6 to 6
- targets: bfloat16 [512, 32, 32, 320], P(('own', 'rep')), may hold values from -6 to 6
- advantages: float32 [512], P(('own', 'rep')), may hold values from -4 to 4
- timesteps: int32 [512], P(('own', 'rep')), may hold values from 0 to 49
- kernel: bfloat16 [2880, 320], replicated, may hold values from -0.109375 to 0.109375
- prior_left: float32 [16, 180, 180], P('own'), as said below
- prior_right: float32 [16, 320, 320], P('own'), as said below
Outputs:
- step: bfloat16 [2880, 320], replicated
The draws below stay inside these ranges and needn't reach their ends.
Inputs may be any that keep to these rules, and one draw needn't show every extreme that they name: `prior_left`: each block is symmetric positive definite. `prior_right`: each block is symmetric positive definite.
All inputs are finite; a program needn't handle non-finite values.
Results may differ from the reference program's by a relative error of at most 0.0049.
Values may be sent and summed in bfloat16 or wider, within the bound.
No kernel may reach another device: no remote copies, remote signals or barrier semaphores. Data moves between devices by JAX's collectives and lax.ppermute only.
A program may use at most 128 MiB of HBM per device.

```python
import jax
import jax.numpy as jnp
from jax import lax

C = 320
BLOCKS = 16
ITERS = 8
STEPS = 50
IMG_H = 32
IMG_W = 32
SAMP_DEV = 2
KROWS = 2880
BROWS = 180
SAMPLES = 512
POSITIONS = 524288


def spd_blocks(key, order, strength):
    base = jax.random.normal(jax.random.fold_in(key, 11), (BLOCKS, order, order), jnp.float32)
    gram = jnp.einsum('bij,bkj->bik', base, base) / order
    identity = jnp.eye(order, dtype=jnp.float32)[None]
    return (gram + 0.5 * identity) * strength


def draw_prior_left(key, part):
    return spd_blocks(jax.random.fold_in(key, 101), BROWS, 40.0 * C / POSITIONS)


def draw_prior_right(key, part):
    return spd_blocks(jax.random.fold_in(key, 202), C, 40.0 * BROWS / POSITIONS)


def plant(array, stream_key, least, largest):
    extent = array.shape
    spot = [jax.random.randint(jax.random.fold_in(stream_key, axis), (), 0, extent[axis]) for axis in range(len(extent))]
    array = array.at[tuple(spot)].set(least)
    longest = extent.index(max(extent))
    spot[longest] = (spot[longest] + 1) % extent[longest]
    return array.at[tuple(spot)].set(largest)


def levels(rng, shape, split, smallest, high):
    def one(dim, shards_of):
        steps = jax.random.uniform(jax.random.fold_in(jax.random.fold_in(rng, 6), dim), (shards_of,), jnp.float32, smallest / len(split), high / len(split))
        return jnp.repeat(jnp.exp(steps), shape[dim] // shards_of).reshape((-1,) + (1,) * (len(shape) - dim - 1))

    loudness = one(*split[0])
    for cut in split[1:]:
        loudness = loudness * one(*cut)
    return loudness


def bell_draw(own_key, extent, width, reach, split=(), kind=jnp.bfloat16):
    array = jax.random.normal(own_key, extent, jnp.float32) * width
    if len(split) > 0:
        array = levels(own_key, extent, split, -0.22, 0.18) * array
    return jnp.clip(array, min=-reach, max=reach).astype(kind)


def setup_inputs(seed: int = 0) -> dict:
    seeds = jax.random.split(jax.random.key(seed), 8)
    return {
        "latents": bell_draw(seeds[0], (SAMPLES, IMG_H, IMG_W, C), 1.0, 6.0, ((0, 256),)),
        "targets": bell_draw(seeds[1], (SAMPLES, IMG_H, IMG_W, C), 1.0, 6.0, ((0, 256),)),
        "advantages": bell_draw(seeds[2], (SAMPLES,), 1.0, 4.0, ((0, 256),), jnp.float32),
        "timesteps": plant(jax.random.randint(seeds[3], (SAMPLES,), 0, STEPS), jax.random.fold_in(seeds[3], 1), 0, STEPS - 1).astype(jnp.int32),
        "kernel": bell_draw(seeds[4], (KROWS, C), KROWS ** -0.5, 0.109375),
        "prior_left": draw_prior_left(jax.random.fold_in(seeds[7], 71), 0),
        "prior_right": draw_prior_right(jax.random.fold_in(seeds[7], 71), 0),
    }


momentum_beta = 0.9

def unfold_taps(images):
    height = images.shape[1]
    breadth = images.shape[2]
    padded = jnp.pad(images, ((0, 0), (1, 1), (1, 1), (0, 0)))
    pieces = [padded[:, row_off:row_off + height, col_off:col_off + breadth, :] for row_off in range(3) for col_off in range(3)]
    stacked = jnp.concatenate(pieces, axis=-1)
    return stacked.reshape(-1, 9 * images.shape[3])

def inverse_root(matrix):
    order = matrix.shape[-1]
    identity = jnp.eye(order, dtype=jnp.float32)[None]
    frob_scale = jnp.sqrt(lax.optimization_barrier(jnp.sum(matrix * matrix, axis=(1, 2), keepdims=True)))
    iterate = matrix / frob_scale
    root_now = jnp.broadcast_to(identity, matrix.shape)
    for sweep in range(ITERS):
        middle = 1.5 * identity - 0.5 * jnp.einsum('bij,bjk->bik', root_now, iterate, precision=lax.Precision.HIGHEST)
        iterate = jnp.einsum('bij,bjk->bik', iterate, middle, precision=lax.Precision.HIGHEST)
        root_now = jnp.einsum('bij,bjk->bik', middle, root_now, precision=lax.Precision.HIGHEST)
    return root_now

def reference(latents, targets, advantages, timesteps, kernel, prior_left, prior_right):
    groups = SAMPLES // SAMP_DEV
    total = float(POSITIONS)
    lat_groups = latents.reshape(groups, SAMP_DEV, IMG_H, IMG_W, C)
    goal_groups = targets.reshape(groups, SAMP_DEV, IMG_H * IMG_W, C)
    adv_groups = advantages.reshape(groups, SAMP_DEV)
    time_groups = timesteps.reshape(groups, SAMP_DEV)

    def accumulate(carry, items):
        images, goals, advant, stamps = items
        columns = unfold_taps(images)
        output = jnp.dot(columns, kernel, preferred_element_type=jnp.float32)
        scaled = advant / ((0.1 + stamps.astype(jnp.float32) / STEPS) * total)
        diffs = output.reshape(SAMP_DEV, IMG_H * IMG_W, C) - goals.astype(jnp.float32)
        cotangent = (scaled[:, None, None] * diffs).astype(jnp.bfloat16).reshape(-1, C)
        grad_term = lax.dot_general(columns, cotangent, (((0,), (0,)), ((), ())), preferred_element_type=jnp.float32)
        return (carry + grad_term, None)
    grad, unused = lax.scan(accumulate, jnp.zeros((KROWS, C), jnp.float32), (lat_groups, goal_groups, adv_groups, time_groups))
    blocks = grad.reshape(BLOCKS, BROWS, C)
    new_left = momentum_beta * prior_left + jnp.einsum('bij,bkj->bik', blocks, blocks, precision=lax.Precision.HIGHEST)
    new_right = momentum_beta * prior_right + jnp.einsum('bji,bjk->bik', blocks, blocks, precision=lax.Precision.HIGHEST)
    root_left = inverse_root(new_left)
    root_right = inverse_root(new_right)
    update = jnp.einsum('bij,bjk->bik', root_left, blocks, precision=lax.Precision.HIGHEST)
    update = jnp.einsum('bij,bjk->bik', update, root_right, precision=lax.Precision.HIGHEST)
    spread_sq = lax.optimization_barrier(jnp.mean(update * update, axis=(1, 2), keepdims=True))
    step = (update / jnp.sqrt(spread_sq + 1e-06)).astype(jnp.bfloat16)
    return step.reshape(KROWS, C)
```

```python
import functools

import jax
import jax.numpy as jnp
from jax import lax
from jax.experimental import pallas as pl
from jax.experimental.pallas import tpu as pltpu
from jax.sharding import PartitionSpec as P

ITERS = 8
STEPS = 50
BETA = 0.9
C = 320
SIDE = 32
SPOTS = 1024
ROWS = 2880
BROWS = 180
BLOCKS = 16
TRIPLE = 3 * C
STRIDE = SPOTS + 2 * SIDE
QROWS = 80
QPACK = 120
bf16 = jnp.bfloat16
f32 = jnp.float32

VMEM = pl.BlockSpec(memory_space=pltpu.VMEM)
SMEM = pl.BlockSpec(memory_space=pltpu.SMEM)


def dot(a, b, contract=(1, 0)):
    return lax.dot_general(
        a, b, (((contract[0],), (contract[1],)), ((), ())), preferred_element_type=f32
    )


def pack_block(block):
    pieces = []
    for q in range(4):
        rows = block[q * QROWS : (q + 1) * QROWS]
        half = QROWS // 2
        tail = jnp.concatenate(
            [
                rows[:half, 128:],
                jnp.zeros((half, 12), block.dtype),
                rows[half:, 128:],
                jnp.zeros((half, 12), block.dtype),
            ],
            axis=1,
        )
        pieces.append((rows[:, :128], tail))
    return pieces


def unpack_quarter(packed):
    half = QROWS // 2
    tail = packed[QROWS:]
    right = jnp.concatenate([tail[:, :52], tail[:, 64:116]], axis=0)
    return jnp.concatenate([packed[:QROWS], right], axis=1)


def conv_kernel(total, core_ref, adv_ref, time_ref, lat_ref, tgt_ref, ker_ref, out_ref, wide, kthree, cot, gt, minus):
    zeros = jnp.zeros((SIDE, TRIPLE), bf16)
    for s in range(2):
        wide[s * STRIDE : s * STRIDE + SIDE, :] = zeros
        wide[s * STRIDE + SIDE + SPOTS : (s + 1) * STRIDE, :] = zeros
    chunk = 128
    column = lax.broadcasted_iota(jnp.int32, (chunk, C), 0) % SIDE

    for s in range(2):

        def widen(i, carry, s=s):
            x = lat_ref[pl.ds(pl.multiple_of(s * SPOTS + i * chunk, chunk), chunk), :].astype(f32)
            before = jnp.where(column == 0, 0.0, pltpu.roll(x, 1, 0))
            after = jnp.where(column == SIDE - 1, 0.0, pltpu.roll(x, chunk - 1, 0))
            row = pl.multiple_of(s * STRIDE + SIDE + i * chunk, 32)
            wide[pl.ds(row, chunk), :] = jnp.concatenate([before, x, after], axis=1).astype(bf16)
            return carry

        lax.fori_loop(0, SPOTS // chunk, widen, 0)
    for a in range(3):
        kthree[a] = ker_ref[:, a * TRIPLE : (a + 1) * TRIPLE]
    rows = lax.broadcasted_iota(jnp.int32, (C, C), 0)
    cols = lax.broadcasted_iota(jnp.int32, (C, C), 1)
    minus[...] = jnp.where(rows == cols, -1.0, 0.0).astype(bf16)

    span = 256
    for s in range(2):
        weight = jnp.full((1, span), adv_ref[s], f32) / (
            (0.1 + jnp.full((1, span), time_ref[s], jnp.int32).astype(f32) / STEPS) * total
        )

        def forward(j, carry, s=s, weight=weight):
            acc = dot(
                minus[...],
                tgt_ref[pl.ds(pl.multiple_of(s * SPOTS + j * span, span), span), :],
                (1, 1),
            )
            for a in range(3):
                row = pl.multiple_of(s * STRIDE + j * span + a * SIDE, 32)
                acc = acc + dot(kthree[a], wide[pl.ds(row, span), :], (1, 1))
            cot[:, pl.ds(pl.multiple_of(s * SPOTS + j * span, span), span)] = (weight * acc).astype(bf16)
            return carry

        lax.fori_loop(0, SPOTS // span, forward, 0)

    for a in range(3):
        for start in range(0, TRIPLE, 256):
            stop = min(start + 256, TRIPLE)
            acc = dot(cot[:, :SPOTS], wide[a * SIDE : a * SIDE + SPOTS, start:stop])
            acc = acc + dot(cot[:, SPOTS:], wide[STRIDE + a * SIDE : STRIDE + a * SIDE + SPOTS, start:stop])
            gt[a, :, start:stop] = acc

    core = core_ref[0]
    for b in range(BLOCKS):
        first, last = b * BROWS, (b + 1) * BROWS
        a = first // TRIPLE
        if last <= (a + 1) * TRIPLE:
            block = gt[a, :, first - a * TRIPLE : last - a * TRIPLE]
        else:
            edge = (a + 1) * TRIPLE
            block = jnp.concatenate(
                [gt[a, :, first - a * TRIPLE : TRIPLE], gt[a + 1, :, 0 : last - edge]], axis=1
            )
        slot = lax.bitwise_xor(core, jnp.int32(b % 2))
        for q, (head, tail) in enumerate(pack_block(block)):
            base = (b // 2) * 4 + q
            out_ref[slot, base, 0:QROWS, :] = head
            out_ref[slot, base, QROWS:QPACK, :] = tail


def conv_grad(total, core, advantages, timesteps, latents, targets, kernel_t):
    return pl.pallas_call(
        functools.partial(conv_kernel, total),
        out_shape=jax.ShapeDtypeStruct((2, 32, QPACK, 128), f32),
        in_specs=[SMEM, SMEM, SMEM, VMEM, VMEM, VMEM],
        out_specs=VMEM,
        scratch_shapes=[
            pltpu.VMEM((2 * STRIDE, TRIPLE), bf16),
            pltpu.VMEM((3, C, TRIPLE), bf16),
            pltpu.VMEM((C, 2 * SPOTS), bf16),
            pltpu.VMEM((3, C, TRIPLE), f32),
            pltpu.VMEM((C, C), bf16),
        ],
        compiler_params=pltpu.CompilerParams(vmem_limit_bytes=40 * 1024 * 1024),
        name="conv_grad",
    )(core, advantages, timesteps, latents, targets, kernel_t)


def halves(x):
    high = x.astype(bf16)
    return high, (x - high.astype(f32)).astype(bf16)


def left_operand(x):
    high, low = halves(x)
    return jnp.concatenate([high, high, low], axis=1)


def right_operand(x):
    high, low = halves(x)
    return jnp.concatenate([high, low, high], axis=0)


def eye(n):
    return jnp.where(
        lax.broadcasted_iota(jnp.int32, (n, n), 0) == lax.broadcasted_iota(jnp.int32, (n, n), 1),
        1.0,
        0.0,
    ).astype(f32)


def unit(matrix):
    total = jnp.sum(jnp.sum(matrix * matrix, axis=1, keepdims=True), axis=0, keepdims=True)
    return matrix / jnp.sqrt(total)


def shampoo_kernel(got_ref, left_ref, right_ref, out_ref, pr, plft, xs):
    quarters = []
    for q in range(4):
        s = got_ref[q].astype(f32)
        for z in range(1, 4):
            s = s + got_ref[4 * z + q].astype(f32)
        quarters.append(unpack_quarter(s))
    h = jnp.concatenate(quarters, axis=0)
    ht = h.T
    xs[...] = h
    pr[...] = unit(BETA * right_ref[...] + dot(left_operand(h), right_operand(ht)))
    plft[...] = unit(BETA * left_ref[...] + dot(left_operand(ht), right_operand(h)))

    def poly(p, square):
        n = p.shape[0]
        return 2.25 * eye(n) - 1.5 * p + 0.25 * square

    def sweep(i, carry):
        p = pr[...]
        x = xs[...]
        p3 = left_operand(p)
        both = dot(p3, right_operand(jnp.concatenate([p, x], axis=1)))
        x = 1.5 * x - 0.5 * both[:, C:]
        pr[...] = dot(p3, right_operand(poly(p, both[:, :C])))
        m = plft[...]
        m3 = right_operand(m)
        both = dot(left_operand(jnp.concatenate([x, m], axis=0)), m3)
        xs[...] = 1.5 * x - 0.5 * both[:C]
        plft[...] = dot(left_operand(m), right_operand(poly(m, both[C:])))
        return carry

    lax.fori_loop(0, ITERS - 1, sweep, 0)
    x = xs[...]
    x = 1.5 * x - 0.5 * dot(left_operand(pr[...]), right_operand(x))
    x = 1.5 * x - 0.5 * dot(left_operand(x), right_operand(plft[...]))
    mean = jnp.sum(jnp.sum(x * x, axis=1, keepdims=True), axis=0, keepdims=True) / (C * BROWS)
    x = x / jnp.sqrt(mean + 1e-06)
    for q, (head, tail) in enumerate(pack_block(x)):
        out_ref[q * QPACK : q * QPACK + QROWS, :] = head.astype(bf16)
        out_ref[q * QPACK + QROWS : (q + 1) * QPACK, :] = tail.astype(bf16)


def shampoo(got, left, right):
    return pl.pallas_call(
        shampoo_kernel,
        out_shape=jax.ShapeDtypeStruct((4 * QPACK, 128), bf16),
        in_specs=[VMEM, VMEM, VMEM],
        out_specs=VMEM,
        scratch_shapes=[
            pltpu.VMEM((C, C), f32),
            pltpu.VMEM((BROWS, BROWS), f32),
            pltpu.VMEM((C, BROWS), f32),
        ],
        compiler_params=pltpu.CompilerParams(vmem_limit_bytes=40 * 1024 * 1024),
        name="shampoo",
    )(got, left, right)


def join_kernel(core_ref, mine_ref, theirs_ref, out_ref):
    core = core_ref[0]

    def write(even, odd):
        for q in range(4):
            pieces = []
            for b in range(BLOCKS):
                source = even if b % 2 == 0 else odd
                packed = source[b // 2, q * QPACK : (q + 1) * QPACK, :].astype(f32)
                pieces.append(unpack_quarter(packed))
            out_ref[q * QROWS : (q + 1) * QROWS, :] = jnp.concatenate(pieces, axis=1).astype(bf16)

    @pl.when(core == 0)
    def _():
        write(mine_ref, theirs_ref)

    @pl.when(core == 1)
    def _():
        write(theirs_ref, mine_ref)


def join(core, mine, theirs):
    return pl.pallas_call(
        join_kernel,
        out_shape=jax.ShapeDtypeStruct((C, ROWS), bf16),
        in_specs=[SMEM, VMEM, VMEM],
        out_specs=VMEM,
        compiler_params=pltpu.CompilerParams(vmem_limit_bytes=40 * 1024 * 1024),
        name="join",
    )(core, mine, theirs)


CORE_SWAP = [(b, b ^ 1) for b in range(16)]
EIGHTS = [[2 * k + c for k in range(8)] for c in range(2)]
WIDE_GROUPS = [
    [(2 * k + c) * 16 + 4 * z + q for k in range(8) for q in range(4)]
    for c in range(2)
    for z in range(4)
]


def local(latents, targets, advantages, timesteps, kernel, prior_left, prior_right):
    core = (lax.axis_index("own") % 2).astype(jnp.int32).reshape(1)
    total = float(2 * SPOTS * lax.axis_size("own") * lax.axis_size("rep"))
    parts = conv_grad(
        total,
        core,
        advantages,
        timesteps,
        latents.reshape(2 * SPOTS, C),
        targets.reshape(2 * SPOTS, C),
        kernel.T,
    )
    theirs = lax.ppermute(parts[1].astype(bf16), "own", CORE_SWAP)
    pair = (parts[0] + theirs.astype(f32)).astype(bf16)
    spread = lax.all_to_all(pair, ("own", "rep"), 0, 0, axis_index_groups=WIDE_GROUPS)
    quarter = jnp.sum(spread.astype(f32), axis=0).astype(bf16)
    got = lax.all_to_all(jnp.broadcast_to(quarter, (16, QPACK, 128)), "rep", 0, 0)
    step = shampoo(got, prior_left[0], prior_right[0])
    mine = lax.all_to_all(
        jnp.broadcast_to(step, (8, 4 * QPACK, 128)), "own", 0, 0, axis_index_groups=EIGHTS
    )
    theirs = lax.ppermute(mine, "own", CORE_SWAP)
    return join(core, mine, theirs).T


def solution(mesh):
    placed = (
        P(("own", "rep"), None, None, None),
        P(("own", "rep"), None, None, None),
        P(("own", "rep")),
        P(("own", "rep")),
        P(),
        P("own", None, None),
        P("own", None, None),
    )
    return jax.shard_map(local, mesh=mesh, in_specs=placed, out_specs=P(), check_vma=False)
```

```python
import functools

import jax
import jax.numpy as jnp
from jax import lax
from jax.experimental import pallas as pl
from jax.experimental.pallas import tpu as pltpu
from jax.sharding import PartitionSpec as P

ITERS = 8
STEPS = 50
BETA = 0.9
C = 320
SIDE = 32
SPOTS = 1024
ROWS = 2880
BROWS = 180
BLOCKS = 16
TRIPLE = 3 * C
STRIDE = SPOTS + 2 * SIDE
QROWS = 80
QPACK = 120
bf16 = jnp.bfloat16
f32 = jnp.float32

VMEM = pl.BlockSpec(memory_space=pltpu.VMEM)
SMEM = pl.BlockSpec(memory_space=pltpu.SMEM)
HBM = pl.BlockSpec(memory_space=pltpu.HBM)


def dot(a, b, contract=(1, 0)):
    return lax.dot_general(
        a, b, (((contract[0],), (contract[1],)), ((), ())), preferred_element_type=f32
    )


def pack_block(block):
    pieces = []
    for q in range(4):
        rows = block[q * QROWS : (q + 1) * QROWS]
        half = QROWS // 2
        tail = jnp.concatenate(
            [
                rows[:half, 128:],
                jnp.zeros((half, 12), block.dtype),
                rows[half:, 128:],
                jnp.zeros((half, 12), block.dtype),
            ],
            axis=1,
        )
        pieces.append((rows[:, :128], tail))
    return pieces


def unpack_quarter(packed):
    half = QROWS // 2
    tail = packed[QROWS:]
    right = jnp.concatenate([tail[:, :52], tail[:, 64:116]], axis=0)
    return jnp.concatenate([packed[:QROWS], right], axis=1)


def conv_kernel(
    total, core_ref, adv_hbm, time_hbm, lat_hbm, tgt_hbm, ker_hbm, out_ref,
    adv, time, lat, tgt, ker, wide, middle, cot, gt, sems,
):
    def fetch(source, target, sem):
        copy = pltpu.make_async_copy(source, target, sems.at[sem])
        copy.start()
        return copy

    half = [pl.ds(s * SPOTS, SPOTS) for s in range(2)]
    get_lat = [fetch(lat_hbm.at[half[0]], lat.at[half[0]], 0)]
    get_ker = fetch(ker_hbm, ker, 1)
    get_adv = fetch(adv_hbm, adv, 2)
    get_time = fetch(time_hbm, time, 3)
    get_tgt = [fetch(tgt_hbm.at[half[0]], tgt.at[half[0]], 4)]
    get_lat.append(fetch(lat_hbm.at[half[1]], lat.at[half[1]], 5))
    get_tgt.append(fetch(tgt_hbm.at[half[1]], tgt.at[half[1]], 6))

    zeros = jnp.zeros((SIDE, TRIPLE), bf16)
    for s in range(2):
        wide[s * STRIDE : s * STRIDE + SIDE, :] = zeros
        wide[s * STRIDE + SIDE + SPOTS : (s + 1) * STRIDE, :] = zeros
    span = 256
    column = lax.broadcasted_iota(jnp.int32, (span, C), 0) % SIDE

    def widen(j):
        s, r = divmod(j * span, SPOTS)
        if r == 0:
            get_lat[s].wait()
        x = lat[j * span : (j + 1) * span, :].astype(f32)
        before = jnp.where(column == 0, 0.0, pltpu.roll(x, 1, 0))
        after = jnp.where(column == SIDE - 1, 0.0, pltpu.roll(x, span - 1, 0))
        row = s * STRIDE + SIDE + r
        wide[row : row + span, :] = jnp.concatenate([before, x, after], axis=1).astype(bf16)

    widen(0)
    widen(1)
    get_ker.wait()
    middle[...] = ker[:, TRIPLE : 2 * TRIPLE]
    get_adv.wait()
    get_time.wait()
    weights = [
        jnp.full((1, span), adv[s], f32)
        / ((0.1 + jnp.full((1, span), time[s], jnp.int32).astype(f32) / STEPS) * total)
        for s in range(2)
    ]
    for j in range(2 * SPOTS // span):
        s, r = divmod(j * span, SPOTS)
        if r == 0:
            get_tgt[s].wait()
        if (j + 2) * span < 2 * SPOTS:
            widen(j + 2)
        row = s * STRIDE + r
        acc = dot(ker[:, :TRIPLE], wide[row : row + span, :], (1, 1))
        acc = acc + dot(middle[...], wide[row + SIDE : row + SIDE + span, :], (1, 1))
        acc = acc + dot(ker[:, 2 * TRIPLE :], wide[row + 2 * SIDE : row + 2 * SIDE + span, :], (1, 1))
        goal = tgt[j * span : (j + 1) * span, :].astype(f32).T
        cot[:, j * span : (j + 1) * span] = (weights[s] * (acc - goal)).astype(bf16)

    for a in range(3):
        for start in range(0, TRIPLE, 256):
            stop = min(start + 256, TRIPLE)
            acc = dot(cot[:, :SPOTS], wide[a * SIDE : a * SIDE + SPOTS, start:stop])
            acc = acc + dot(cot[:, SPOTS:], wide[STRIDE + a * SIDE : STRIDE + a * SIDE + SPOTS, start:stop])
            gt[a, :, start:stop] = acc

    core = core_ref[0]
    for b in range(BLOCKS):
        first, last = b * BROWS, (b + 1) * BROWS
        a = first // TRIPLE
        if last <= (a + 1) * TRIPLE:
            block = gt[a, :, first - a * TRIPLE : last - a * TRIPLE]
        else:
            edge = (a + 1) * TRIPLE
            block = jnp.concatenate(
                [gt[a, :, first - a * TRIPLE : TRIPLE], gt[a + 1, :, 0 : last - edge]], axis=1
            )
        slot = lax.bitwise_xor(core, jnp.int32(b % 2))
        for q, (head, tail) in enumerate(pack_block(block)):
            base = (b // 2) * 4 + q
            out_ref[slot, base, 0:QROWS, :] = head
            out_ref[slot, base, QROWS:QPACK, :] = tail


def conv_grad(total, core, advantages, timesteps, latents, targets, kernel_t):
    return pl.pallas_call(
        functools.partial(conv_kernel, total),
        out_shape=jax.ShapeDtypeStruct((2, 32, QPACK, 128), f32),
        in_specs=[SMEM, HBM, HBM, HBM, HBM, HBM],
        out_specs=VMEM,
        scratch_shapes=[
            pltpu.SMEM((2,), f32),
            pltpu.SMEM((2,), jnp.int32),
            pltpu.VMEM((2 * SPOTS, C), bf16),
            pltpu.VMEM((2 * SPOTS, C), bf16),
            pltpu.VMEM((C, ROWS), bf16),
            pltpu.VMEM((2 * STRIDE, TRIPLE), bf16),
            pltpu.VMEM((C, TRIPLE), bf16),
            pltpu.VMEM((C, 2 * SPOTS), bf16),
            pltpu.VMEM((3, C, TRIPLE), f32),
            pltpu.SemaphoreType.DMA((7,)),
        ],
        compiler_params=pltpu.CompilerParams(vmem_limit_bytes=50 * 1024 * 1024),
        name="conv_grad",
    )(core, advantages, timesteps, latents, targets, kernel_t)


def halves(x):
    high = x.astype(bf16)
    return high, (x - high.astype(f32)).astype(bf16)


def left_operand(x):
    high, low = halves(x)
    return jnp.concatenate([high, high, low], axis=1)


def right_operand(x):
    high, low = halves(x)
    return jnp.concatenate([high, low, high], axis=0)


def eye(n):
    return jnp.where(
        lax.broadcasted_iota(jnp.int32, (n, n), 0) == lax.broadcasted_iota(jnp.int32, (n, n), 1),
        1.0,
        0.0,
    ).astype(f32)


def unit(matrix):
    total = jnp.sum(jnp.sum(matrix * matrix, axis=1, keepdims=True), axis=0, keepdims=True)
    return matrix / jnp.sqrt(total)


def shampoo_kernel(got_ref, left_ref, right_ref, out_ref, pr, plft, xs):
    quarters = []
    for q in range(4):
        quarters.append(unpack_quarter(got_ref[q].astype(f32)))
    h = jnp.concatenate(quarters, axis=0)
    ht = h.T
    xs[...] = h
    pr[...] = unit(BETA * right_ref[...] + dot(left_operand(h), right_operand(ht)))
    plft[...] = unit(BETA * left_ref[...] + dot(left_operand(ht), right_operand(h)))

    def poly(p, square):
        n = p.shape[0]
        return 2.25 * eye(n) - 1.5 * p + 0.25 * square

    def sweep(i, carry):
        p = pr[...]
        x = xs[...]
        p3 = left_operand(p)
        both = dot(p3, right_operand(jnp.concatenate([p, x], axis=1)))
        x = 1.5 * x - 0.5 * both[:, C:]
        pr[...] = dot(p3, right_operand(poly(p, both[:, :C])))
        m = plft[...]
        m3 = right_operand(m)
        both = dot(left_operand(jnp.concatenate([x, m], axis=0)), m3)
        xs[...] = 1.5 * x - 0.5 * both[:C]
        plft[...] = dot(left_operand(m), right_operand(poly(m, both[C:])))
        return carry

    lax.fori_loop(0, ITERS - 1, sweep, 0)
    x = xs[...]
    x = 1.5 * x - 0.5 * dot(left_operand(pr[...]), right_operand(x))
    x = 1.5 * x - 0.5 * dot(left_operand(x), right_operand(plft[...]))
    mean = jnp.sum(jnp.sum(x * x, axis=1, keepdims=True), axis=0, keepdims=True) / (C * BROWS)
    x = x / jnp.sqrt(mean + 1e-06)
    for q, (head, tail) in enumerate(pack_block(x)):
        out_ref[q * QPACK : q * QPACK + QROWS, :] = head.astype(bf16)
        out_ref[q * QPACK + QROWS : (q + 1) * QPACK, :] = tail.astype(bf16)


def shampoo(got, left, right):
    return pl.pallas_call(
        shampoo_kernel,
        out_shape=jax.ShapeDtypeStruct((4 * QPACK, 128), bf16),
        in_specs=[VMEM, VMEM, VMEM],
        out_specs=VMEM,
        scratch_shapes=[
            pltpu.VMEM((C, C), f32),
            pltpu.VMEM((BROWS, BROWS), f32),
            pltpu.VMEM((C, BROWS), f32),
        ],
        compiler_params=pltpu.CompilerParams(vmem_limit_bytes=40 * 1024 * 1024),
        name="shampoo",
    )(got, left, right)


def join_kernel(core_ref, mine_ref, theirs_ref, out_ref):
    core = core_ref[0]

    def write(even, odd):
        for q in range(4):
            pieces = []
            for b in range(BLOCKS):
                source = even if b % 2 == 0 else odd
                packed = source[b // 2, q * QPACK : (q + 1) * QPACK, :].astype(f32)
                pieces.append(unpack_quarter(packed))
            out_ref[q * QROWS : (q + 1) * QROWS, :] = jnp.concatenate(pieces, axis=1).astype(bf16)

    @pl.when(core == 0)
    def _():
        write(mine_ref, theirs_ref)

    @pl.when(core == 1)
    def _():
        write(theirs_ref, mine_ref)


def join(core, mine, theirs):
    return pl.pallas_call(
        join_kernel,
        out_shape=jax.ShapeDtypeStruct((C, ROWS), bf16),
        in_specs=[SMEM, VMEM, VMEM],
        out_specs=VMEM,
        compiler_params=pltpu.CompilerParams(vmem_limit_bytes=40 * 1024 * 1024),
        name="join",
    )(core, mine, theirs)


CORE_SWAP = [(b, b ^ 1) for b in range(16)]
EIGHTS = [[2 * k + c for k in range(8)] for c in range(2)]
WIDE_GROUPS = [
    [(2 * k + c) * 16 + 4 * z + q for k in range(8) for q in range(4)]
    for c in range(2)
    for z in range(4)
]
FAR_GROUPS = [[4 * z + q for z in range(4)] for q in range(4)]
NEAR_GROUPS = [[4 * z + q for q in range(4)] for z in range(4)]


def local(latents, targets, advantages, timesteps, kernel, prior_left, prior_right):
    core = (lax.axis_index("own") % 2).astype(jnp.int32).reshape(1)
    total = float(2 * SPOTS * lax.axis_size("own") * lax.axis_size("rep"))
    parts = conv_grad(
        total,
        core,
        advantages,
        timesteps,
        latents.reshape(2 * SPOTS, C),
        targets.reshape(2 * SPOTS, C),
        kernel.T,
    )
    theirs = lax.ppermute(parts[1].astype(bf16), "own", CORE_SWAP)
    pair = (parts[0] + theirs.astype(f32)).astype(bf16)
    spread = lax.all_to_all(pair, ("own", "rep"), 0, 0, axis_index_groups=WIDE_GROUPS)
    quarter = lax.optimization_barrier(jnp.sum(spread.astype(f32), axis=0)).astype(bf16)
    far = lax.all_to_all(
        jnp.broadcast_to(quarter, (4, QPACK, 128)), "rep", 0, 0, axis_index_groups=FAR_GROUPS
    )
    quarter = lax.optimization_barrier(jnp.sum(far.astype(f32), axis=0)).astype(bf16)
    got = lax.all_to_all(
        jnp.broadcast_to(quarter, (4, QPACK, 128)), "rep", 0, 0, axis_index_groups=NEAR_GROUPS
    )
    step = shampoo(got, prior_left[0], prior_right[0])
    mine = lax.all_to_all(
        jnp.broadcast_to(step, (8, 4 * QPACK, 128)), "own", 0, 0, axis_index_groups=EIGHTS
    )
    theirs = lax.ppermute(mine, "own", CORE_SWAP)
    return join(core, mine, theirs).T


def solution(mesh):
    placed = (
        P(("own", "rep"), None, None, None),
        P(("own", "rep"), None, None, None),
        P(("own", "rep")),
        P(("own", "rep")),
        P(),
        P("own", None, None),
        P("own", None, None),
    )
    return jax.shard_map(local, mesh=mesh, in_specs=placed, out_specs=P(), check_vma=False)
```

```python
import functools

import jax
import jax.numpy as jnp
from jax import lax
from jax.experimental import pallas as pl
from jax.experimental.pallas import tpu as pltpu
from jax.sharding import PartitionSpec as P

ITERS = 8
STEPS = 50
BETA = 0.9
C = 320
SIDE = 32
SPOTS = 1024
ROWS = 2880
BROWS = 180
BLOCKS = 16
TRIPLE = 3 * C
STRIDE = SPOTS + 2 * SIDE
QROWS = 80
QPACK = 120
bf16 = jnp.bfloat16
f32 = jnp.float32

VMEM = pl.BlockSpec(memory_space=pltpu.VMEM)
SMEM = pl.BlockSpec(memory_space=pltpu.SMEM)
HBM = pl.BlockSpec(memory_space=pltpu.HBM)


def dot(a, b, contract=(1, 0)):
    return lax.dot_general(
        a, b, (((contract[0],), (contract[1],)), ((), ())), preferred_element_type=f32
    )


def pack_block(block):
    pieces = []
    for q in range(4):
        rows = block[q * QROWS : (q + 1) * QROWS]
        half = QROWS // 2
        tail = jnp.concatenate(
            [
                rows[:half, 128:],
                jnp.zeros((half, 12), block.dtype),
                rows[half:, 128:],
                jnp.zeros((half, 12), block.dtype),
            ],
            axis=1,
        )
        pieces.append((rows[:, :128], tail))
    return pieces


def unpack_quarter(packed):
    half = QROWS // 2
    tail = packed[QROWS:]
    right = jnp.concatenate([tail[:, :52], tail[:, 64:116]], axis=0)
    return jnp.concatenate([packed[:QROWS], right], axis=1)


def conv_kernel(
    total, core_ref, adv_hbm, time_hbm, lat_hbm, tgt_hbm, ker_hbm, mine_ref, theirs_ref,
    adv, time, lat, tgt, ker, wide, middle, cot, gt, sems,
):
    def fetch(source, target, sem):
        copy = pltpu.make_async_copy(source, target, sems.at[sem])
        copy.start()
        return copy

    def rows(first, last):
        return pl.ds(first, last - first)

    def columns(first, last):
        return (slice(None), rows(first, last))

    first, half, end = 512, SPOTS, 2 * SPOTS
    get_lat = {0: fetch(lat_hbm.at[rows(0, first)], lat.at[rows(0, first)], 0)}
    cuts = (0, 1024, 1920, ROWS)
    get_ker = [
        fetch(ker_hbm.at[columns(i, j)], ker.at[columns(i, j)], 1 + n)
        for n, (i, j) in enumerate(zip(cuts, cuts[1:]))
    ]
    get_adv = fetch(adv_hbm, adv, 4)
    get_time = fetch(time_hbm, time, 5)
    get_tgt = [fetch(tgt_hbm.at[rows(0, half)], tgt.at[rows(0, half)], 6)]
    get_lat[first] = fetch(lat_hbm.at[rows(first, half)], lat.at[rows(first, half)], 7)
    get_lat[half] = fetch(lat_hbm.at[rows(half, end)], lat.at[rows(half, end)], 8)
    get_tgt.append(fetch(tgt_hbm.at[rows(half, end)], tgt.at[rows(half, end)], 9))

    zeros = jnp.zeros((SIDE, TRIPLE), bf16)
    for s in range(2):
        wide[s * STRIDE : s * STRIDE + SIDE, :] = zeros
        wide[s * STRIDE + SIDE + SPOTS : (s + 1) * STRIDE, :] = zeros
    span = 256
    column = lax.broadcasted_iota(jnp.int32, (span, C), 0) % SIDE

    def widen(j):
        s, r = divmod(j * span, SPOTS)
        if j * span in get_lat:
            get_lat[j * span].wait()
        x = lat[j * span : (j + 1) * span, :].astype(f32)
        before = jnp.where(column == 0, 0.0, pltpu.roll(x, 1, 0))
        after = jnp.where(column == SIDE - 1, 0.0, pltpu.roll(x, span - 1, 0))
        row = s * STRIDE + SIDE + r
        wide[row : row + span, :] = jnp.concatenate([before, x, after], axis=1).astype(bf16)

    widen(0)
    widen(1)
    for copy in get_ker:
        copy.wait()
    middle[...] = ker[:, TRIPLE : 2 * TRIPLE]
    get_adv.wait()
    get_time.wait()
    weights = [
        jnp.full((1, span), adv[s], f32)
        / ((0.1 + jnp.full((1, span), time[s], jnp.int32).astype(f32) / STEPS) * total)
        for s in range(2)
    ]
    for j in range(2 * SPOTS // span):
        s, r = divmod(j * span, SPOTS)
        if r == 0:
            get_tgt[s].wait()
        if (j + 2) * span < 2 * SPOTS:
            widen(j + 2)
        row = s * STRIDE + r
        acc = dot(ker[:, :TRIPLE], wide[row : row + span, :], (1, 1))
        acc = acc + dot(middle[...], wide[row + SIDE : row + SIDE + span, :], (1, 1))
        acc = acc + dot(ker[:, 2 * TRIPLE :], wide[row + 2 * SIDE : row + 2 * SIDE + span, :], (1, 1))
        goal = tgt[j * span : (j + 1) * span, :].astype(f32).T
        cot[:, j * span : (j + 1) * span] = (weights[s] * (acc - goal)).astype(bf16)

    for a in range(3):
        for start in range(0, TRIPLE, 256):
            stop = min(start + 256, TRIPLE)
            acc = dot(cot[:, :SPOTS], wide[a * SIDE : a * SIDE + SPOTS, start:stop])
            acc = acc + dot(cot[:, SPOTS:], wide[STRIDE + a * SIDE : STRIDE + a * SIDE + SPOTS, start:stop])
            gt[a, :, start:stop] = acc

    def block(b):
        first, last = b * BROWS, (b + 1) * BROWS
        a = first // TRIPLE
        if last <= (a + 1) * TRIPLE:
            return gt[a, :, first - a * TRIPLE : last - a * TRIPLE]
        edge = (a + 1) * TRIPLE
        return jnp.concatenate([gt[a, :, first - a * TRIPLE : TRIPLE], gt[a + 1, :, 0 : last - edge]], axis=1)

    even_core = core_ref[0] == 0
    for k in range(BLOCKS // 2):
        even, odd = block(2 * k), block(2 * k + 1)
        for q, (head, tail) in enumerate(pack_block(jnp.where(even_core, even, odd))):
            mine_ref[8 * q + k, 0:QROWS, :] = head
            mine_ref[8 * q + k, QROWS:QPACK, :] = tail
        for q, (head, tail) in enumerate(pack_block(jnp.where(even_core, odd, even))):
            theirs_ref[8 * q + k, 0:QROWS, :] = head.astype(bf16)
            theirs_ref[8 * q + k, QROWS:QPACK, :] = tail.astype(bf16)


def conv_grad(total, core, advantages, timesteps, latents, targets, kernel_t):
    return pl.pallas_call(
        functools.partial(conv_kernel, total),
        out_shape=(
            jax.ShapeDtypeStruct((32, QPACK, 128), f32),
            jax.ShapeDtypeStruct((32, QPACK, 128), bf16),
        ),
        in_specs=[SMEM, HBM, HBM, HBM, HBM, HBM],
        out_specs=(VMEM, VMEM),
        scratch_shapes=[
            pltpu.SMEM((2,), f32),
            pltpu.SMEM((2,), jnp.int32),
            pltpu.VMEM((2 * SPOTS, C), bf16),
            pltpu.VMEM((2 * SPOTS, C), bf16),
            pltpu.VMEM((C, ROWS), bf16),
            pltpu.VMEM((2 * STRIDE, TRIPLE), bf16),
            pltpu.VMEM((C, TRIPLE), bf16),
            pltpu.VMEM((C, 2 * SPOTS), bf16),
            pltpu.VMEM((3, C, TRIPLE), f32),
            pltpu.SemaphoreType.DMA((10,)),
        ],
        compiler_params=pltpu.CompilerParams(vmem_limit_bytes=28 * 1024 * 1024),
        name="conv_grad",
    )(core, *(pltpu.with_memory_space_constraint(x, pltpu.HBM) for x in (advantages, timesteps, latents, targets, kernel_t)))


def halves(x):
    high = x.astype(bf16)
    return high, (x - high.astype(f32)).astype(bf16)


def left_operand(x):
    high, low = halves(x)
    return jnp.concatenate([high, high, low], axis=1)


def right_operand(x):
    high, low = halves(x)
    return jnp.concatenate([high, low, high], axis=0)


def eye(n):
    return jnp.where(
        lax.broadcasted_iota(jnp.int32, (n, n), 0) == lax.broadcasted_iota(jnp.int32, (n, n), 1),
        1.0,
        0.0,
    ).astype(f32)


def unit(matrix):
    total = jnp.sum(jnp.sum(matrix * matrix, axis=1, keepdims=True), axis=0, keepdims=True)
    return matrix * (1.0 / jnp.sqrt(total))


def shampoo_kernel(got_ref, left_ref, right_ref, out_ref, pr, plft, xs, zl):
    quarters = []
    for q in range(4):
        quarters.append(unpack_quarter(got_ref[q].astype(f32)))
    h = jnp.concatenate(quarters, axis=0)
    ht = h.T
    xs[...] = h
    zl[...] = eye(BROWS)
    pr[...] = unit(right_ref[...] + dot(left_operand(h), right_operand(ht)))
    plft[...] = unit(left_ref[...] + dot(left_operand(ht), right_operand(h)))

    def sweep(i, carry):
        p = pr[...]
        x = xs[...]
        (ph, pl_), (xh, xl) = halves(p), halves(x)
        p3 = jnp.concatenate([ph, ph, pl_], axis=1)
        high = jnp.concatenate([ph, xh], axis=1)
        both = dot(p3, jnp.concatenate([high, jnp.concatenate([pl_, xl], axis=1), high], axis=0))
        xs[...] = 1.5 * x - 0.5 * both[:, C:]
        q3 = right_operand(0.25 * both[:, :C] - 1.5 * p)
        body = 2.25 * p[:, :256] + dot(p3, q3[:, :256])
        pr[:, :256] = body
        pr[:256, 256:] = body[256:].T
        pr[256:, 256:] = 2.25 * p[256:, 256:] + dot(p3[256:], q3[:, 256:])
        m = plft[...]
        mh, ml = halves(m)
        m3 = jnp.concatenate([mh, ml, mh], axis=0)
        left = jnp.concatenate([mh, mh, ml], axis=1)
        square = dot(left, m3)
        z = zl[...]
        zl[...] = 1.5 * z - 0.5 * dot(left_operand(z), m3)
        plft[...] = 2.25 * m + dot(left, right_operand(0.25 * square - 1.5 * m))
        return carry

    for _ in range(ITERS - 2):
        sweep(0, 0)
    x = xs[...]
    z = zl[...]
    d = (eye(C) - pr[...]).astype(bf16)
    e = (eye(BROWS) - plft[...]).astype(bf16)
    square = dot(e, e)
    z = z + 0.5 * dot(z.astype(bf16), e)
    e = (0.75 * square + 0.25 * dot(e, square.astype(bf16))).astype(bf16)
    z = z + 0.5 * dot(z.astype(bf16), e)
    both = dot(d, jnp.concatenate([d, x.astype(bf16)], axis=1))
    x = x + 0.5 * both[:, C:]
    square = both[:, :C]
    d = (0.75 * square + 0.25 * dot(d, square.astype(bf16))).astype(bf16)
    x = x + 0.5 * dot(d, x.astype(bf16))
    x = dot(left_operand(x), right_operand(z))
    mean = jnp.sum(jnp.sum(x * x, axis=1, keepdims=True), axis=0, keepdims=True) / (C * BROWS)
    x = x * (1.0 / jnp.sqrt(mean + 1e-06))
    for q, (head, tail) in enumerate(pack_block(x)):
        out_ref[q * QPACK : q * QPACK + QROWS, :] = head.astype(bf16)
        out_ref[q * QPACK + QROWS : (q + 1) * QPACK, :] = tail.astype(bf16)


def shampoo(got, left, right):
    return pl.pallas_call(
        shampoo_kernel,
        out_shape=jax.ShapeDtypeStruct((4 * QPACK, 128), bf16),
        in_specs=[VMEM, VMEM, VMEM],
        out_specs=VMEM,
        scratch_shapes=[
            pltpu.VMEM((C, C), f32),
            pltpu.VMEM((BROWS, BROWS), f32),
            pltpu.VMEM((C, BROWS), f32),
            pltpu.VMEM((BROWS, BROWS), f32),
        ],
        compiler_params=pltpu.CompilerParams(vmem_limit_bytes=40 * 1024 * 1024),
        name="shampoo",
    )(got, left, right)


def placed(source, q, parity):
    blank = jnp.zeros((QROWS, BROWS), bf16)
    pieces = []
    for k in range(BLOCKS // 2):
        block = unpack_quarter(source[LAST_ORDER.index(k), q * QPACK : (q + 1) * QPACK, :])
        pieces += [block, blank] if parity == 0 else [blank, block]
    return jnp.concatenate(pieces, axis=1)


def place_kernel(core_ref, mine_ref, out_ref):
    for parity in range(2):

        @pl.when(core_ref[0] == parity)
        def _(parity=parity):
            for q in range(4):
                out_ref[q * QROWS : (q + 1) * QROWS, :] = placed(mine_ref, q, parity)


def join_kernel(core_ref, part_ref, theirs_ref, out_hbm, full, sems):
    def copy(q):
        rows = pl.ds(q * QROWS, QROWS)
        return pltpu.make_async_copy(full.at[rows], out_hbm.at[rows], sems.at[q])

    for parity in range(2):

        @pl.when(core_ref[0] == parity)
        def _(parity=parity):
            for q in range(4):
                rows = slice(q * QROWS, (q + 1) * QROWS)
                full[rows, :] = part_ref[rows, :] + placed(theirs_ref, q, 1 - parity)
                copy(q).start()

    for q in range(4):
        copy(q).wait()


def place(core, mine):
    return pl.pallas_call(
        place_kernel,
        out_shape=jax.ShapeDtypeStruct((C, ROWS), bf16),
        in_specs=[SMEM, VMEM],
        out_specs=VMEM,
        compiler_params=pltpu.CompilerParams(vmem_limit_bytes=20 * 1024 * 1024),
        cost_estimate=pl.CostEstimate(flops=4000000, bytes_accessed=4000000, transcendentals=0),
        name="place",
    )(core, mine)


def join(core, part, theirs):
    return pl.pallas_call(
        join_kernel,
        out_shape=jax.ShapeDtypeStruct((C, ROWS), bf16),
        in_specs=[SMEM, VMEM, VMEM],
        out_specs=HBM,
        scratch_shapes=[pltpu.VMEM((C, ROWS), bf16), pltpu.SemaphoreType.DMA((4,))],
        compiler_params=pltpu.CompilerParams(vmem_limit_bytes=20 * 1024 * 1024),
        name="join",
    )(core, part, theirs)


CORE_SWAP = [(b, b ^ 1) for b in range(16)]
LAST_ORDER = (1, 4, 3, 6, 0, 5, 7, 2)
EIGHTS = [
    [(8 * (k // 4) + 2 * (k % 4) + c) * 16 + 2 * z + ((k // 4) ^ p) for k in LAST_ORDER]
    for c in range(2)
    for z in range(8)
    for p in range(2)
]
WIDE_GROUPS = [
    [(2 * k + c) * 16 + 4 * z + q for q in range(4) for k in range(8)]
    for c in range(2)
    for z in range(4)
]
FAR_GROUPS = [[4 * z + q for z in range(4)] for q in range(4)]
NEAR_GROUPS = [[4 * z + q for q in range(4)] for z in range(4)]


def local(latents, targets, advantages, timesteps, kernel, prior_left, prior_right):
    core = (lax.axis_index("own") % 2).astype(jnp.int32).reshape(1)
    total = float(2 * SPOTS * lax.axis_size("own") * lax.axis_size("rep"))
    mine, theirs = conv_grad(
        total,
        core,
        advantages,
        timesteps,
        latents.reshape(2 * SPOTS, C),
        targets.reshape(2 * SPOTS, C),
        kernel.T,
    )
    theirs = lax.ppermute(theirs, "own", CORE_SWAP)
    pair = (mine + theirs.astype(f32)).astype(bf16)
    pair, left, right = lax.optimization_barrier((pair, BETA * prior_left[0], BETA * prior_right[0]))
    spread = lax.all_to_all(pair, ("own", "rep"), 0, 0, axis_index_groups=WIDE_GROUPS)
    quarter = lax.optimization_barrier(jnp.sum(spread.astype(f32), axis=0)).astype(bf16)
    far = lax.all_to_all(
        jnp.broadcast_to(quarter, (4, QPACK, 128)), "rep", 0, 0, axis_index_groups=FAR_GROUPS
    )
    quarter = lax.optimization_barrier(jnp.sum(far.astype(f32), axis=0)).astype(bf16)
    got = lax.all_to_all(
        jnp.broadcast_to(quarter, (4, QPACK, 128)), "rep", 0, 0, axis_index_groups=NEAR_GROUPS
    )
    step = shampoo(got, left, right)
    mine = lax.all_to_all(
        jnp.broadcast_to(step, (8, 4 * QPACK, 128)), ("own", "rep"), 0, 0, axis_index_groups=EIGHTS
    )
    theirs = lax.ppermute(mine, "own", CORE_SWAP)
    return join(core, place(core, mine), theirs).T


def solution(mesh):
    placed = (
        P(("own", "rep"), None, None, None),
        P(("own", "rep"), None, None, None),
        P(("own", "rep")),
        P(("own", "rep")),
        P(),
        P("own", None, None),
        P("own", None, None),
    )
    return jax.shard_map(local, mesh=mesh, in_specs=placed, out_specs=P(), check_vma=False)
```

```python
import functools

import jax
import jax.numpy as jnp
from jax import lax
from jax.experimental import pallas as pl
from jax.experimental.pallas import tpu as pltpu
from jax.sharding import PartitionSpec as P

ITERS = 8
STEPS = 50
BETA = 0.9
C = 320
SIDE = 32
SPOTS = 1024
ROWS = 2880
BROWS = 180
BLOCKS = 16
TRIPLE = 3 * C
STRIDE = SPOTS + 2 * SIDE
QROWS = 80
QPACK = 120
bf16 = jnp.bfloat16
f32 = jnp.float32

VMEM = pl.BlockSpec(memory_space=pltpu.VMEM)
SMEM = pl.BlockSpec(memory_space=pltpu.SMEM)
HBM = pl.BlockSpec(memory_space=pltpu.HBM)


def dot(a, b, contract=(1, 0)):
    return lax.dot_general(
        a, b, (((contract[0],), (contract[1],)), ((), ())), preferred_element_type=f32
    )


def pack_block(block):
    pieces = []
    for q in range(4):
        rows = block[q * QROWS : (q + 1) * QROWS]
        half = QROWS // 2
        tail = jnp.concatenate(
            [
                rows[:half, 128:],
                jnp.zeros((half, 12), block.dtype),
                rows[half:, 128:],
                jnp.zeros((half, 12), block.dtype),
            ],
            axis=1,
        )
        pieces.append((rows[:, :128], tail))
    return pieces


def unpack_quarter(packed):
    half = QROWS // 2
    tail = packed[QROWS:]
    right = jnp.concatenate([tail[:, :52], tail[:, 64:116]], axis=0)
    return jnp.concatenate([packed[:QROWS], right], axis=1)


def conv_kernel(
    total, core_ref, adv_hbm, time_hbm, lat_hbm, tgt_hbm, ker_hbm, mine_ref, theirs_ref,
    adv, time, lat, tgt, ker, wide, middle, cot, gt, sems,
):
    def fetch(source, target, sem):
        copy = pltpu.make_async_copy(source, target, sems.at[sem])
        copy.start()
        return copy

    def rows(first, last):
        return pl.ds(first, last - first)

    def columns(first, last):
        return (slice(None), rows(first, last))

    first, half, end = 512, SPOTS, 2 * SPOTS
    get_lat = {0: fetch(lat_hbm.at[rows(0, first)], lat.at[rows(0, first)], 0)}
    cuts = (0, 1024, 1920, ROWS)
    get_ker = [
        fetch(ker_hbm.at[columns(i, j)], ker.at[columns(i, j)], 1 + n)
        for n, (i, j) in enumerate(zip(cuts, cuts[1:]))
    ]
    get_adv = fetch(adv_hbm, adv, 4)
    get_time = fetch(time_hbm, time, 5)
    get_tgt = [fetch(tgt_hbm.at[rows(0, half)], tgt.at[rows(0, half)], 6)]
    get_lat[first] = fetch(lat_hbm.at[rows(first, half)], lat.at[rows(first, half)], 7)
    get_lat[half] = fetch(lat_hbm.at[rows(half, end)], lat.at[rows(half, end)], 8)
    get_tgt.append(fetch(tgt_hbm.at[rows(half, end)], tgt.at[rows(half, end)], 9))

    zeros = jnp.zeros((SIDE, TRIPLE), bf16)
    for s in range(2):
        wide[s * STRIDE : s * STRIDE + SIDE, :] = zeros
        wide[s * STRIDE + SIDE + SPOTS : (s + 1) * STRIDE, :] = zeros
    span = 256
    column = lax.broadcasted_iota(jnp.int32, (span, C), 0) % SIDE

    def widen(j):
        s, r = divmod(j * span, SPOTS)
        if j * span in get_lat:
            get_lat[j * span].wait()
        x = lat[j * span : (j + 1) * span, :].astype(f32)
        before = jnp.where(column == 0, 0.0, pltpu.roll(x, 1, 0))
        after = jnp.where(column == SIDE - 1, 0.0, pltpu.roll(x, span - 1, 0))
        row = s * STRIDE + SIDE + r
        wide[row : row + span, :] = jnp.concatenate([before, x, after], axis=1).astype(bf16)

    widen(0)
    widen(1)
    for copy in get_ker:
        copy.wait()
    middle[...] = ker[:, TRIPLE : 2 * TRIPLE]
    get_adv.wait()
    get_time.wait()
    weights = [
        jnp.full((1, span), adv[s], f32)
        / ((0.1 + jnp.full((1, span), time[s], jnp.int32).astype(f32) / STEPS) * total)
        for s in range(2)
    ]
    for j in range(2 * SPOTS // span):
        s, r = divmod(j * span, SPOTS)
        if r == 0:
            get_tgt[s].wait()
        if (j + 2) * span < 2 * SPOTS:
            widen(j + 2)
        row = s * STRIDE + r
        acc = dot(ker[:, :TRIPLE], wide[row : row + span, :], (1, 1))
        acc = acc + dot(middle[...], wide[row + SIDE : row + SIDE + span, :], (1, 1))
        acc = acc + dot(ker[:, 2 * TRIPLE :], wide[row + 2 * SIDE : row + 2 * SIDE + span, :], (1, 1))
        goal = tgt[j * span : (j + 1) * span, :].astype(f32).T
        cot[:, j * span : (j + 1) * span] = (weights[s] * (acc - goal)).astype(bf16)

    for a in range(3):
        for start in range(0, TRIPLE, 256):
            stop = min(start + 256, TRIPLE)
            acc = dot(cot[:, :SPOTS], wide[a * SIDE : a * SIDE + SPOTS, start:stop])
            acc = acc + dot(cot[:, SPOTS:], wide[STRIDE + a * SIDE : STRIDE + a * SIDE + SPOTS, start:stop])
            gt[a, :, start:stop] = acc

    def block(b):
        first, last = b * BROWS, (b + 1) * BROWS
        a = first // TRIPLE
        if last <= (a + 1) * TRIPLE:
            return gt[a, :, first - a * TRIPLE : last - a * TRIPLE]
        edge = (a + 1) * TRIPLE
        return jnp.concatenate([gt[a, :, first - a * TRIPLE : TRIPLE], gt[a + 1, :, 0 : last - edge]], axis=1)

    even_core = core_ref[0] == 0
    for k in range(BLOCKS // 2):
        even, odd = block(2 * k), block(2 * k + 1)
        for q, (head, tail) in enumerate(pack_block(jnp.where(even_core, even, odd))):
            mine_ref[8 * q + k, 0:QROWS, :] = head
            mine_ref[8 * q + k, QROWS:QPACK, :] = tail
        for q, (head, tail) in enumerate(pack_block(jnp.where(even_core, odd, even))):
            theirs_ref[8 * q + k, 0:QROWS, :] = head.astype(bf16)
            theirs_ref[8 * q + k, QROWS:QPACK, :] = tail.astype(bf16)


def conv_grad(total, core, advantages, timesteps, latents, targets, kernel_t):
    return pl.pallas_call(
        functools.partial(conv_kernel, total),
        out_shape=(
            jax.ShapeDtypeStruct((32, QPACK, 128), f32),
            jax.ShapeDtypeStruct((32, QPACK, 128), bf16),
        ),
        in_specs=[SMEM, HBM, HBM, HBM, HBM, HBM],
        out_specs=(VMEM, VMEM),
        scratch_shapes=[
            pltpu.SMEM((2,), f32),
            pltpu.SMEM((2,), jnp.int32),
            pltpu.VMEM((2 * SPOTS, C), bf16),
            pltpu.VMEM((2 * SPOTS, C), bf16),
            pltpu.VMEM((C, ROWS), bf16),
            pltpu.VMEM((2 * STRIDE, TRIPLE), bf16),
            pltpu.VMEM((C, TRIPLE), bf16),
            pltpu.VMEM((C, 2 * SPOTS), bf16),
            pltpu.VMEM((3, C, TRIPLE), f32),
            pltpu.SemaphoreType.DMA((10,)),
        ],
        compiler_params=pltpu.CompilerParams(vmem_limit_bytes=28 * 1024 * 1024),
        name="conv_grad",
    )(core, *(pltpu.with_memory_space_constraint(x, pltpu.HBM) for x in (advantages, timesteps, latents, targets, kernel_t)))


def halves(x):
    high = x.astype(bf16)
    return high, (x - high.astype(f32)).astype(bf16)


def left_operand(x):
    high, low = halves(x)
    return jnp.concatenate([high, high, low], axis=1)


def right_operand(x):
    high, low = halves(x)
    return jnp.concatenate([high, low, high], axis=0)


def eye(n):
    return jnp.where(
        lax.broadcasted_iota(jnp.int32, (n, n), 0) == lax.broadcasted_iota(jnp.int32, (n, n), 1),
        1.0,
        0.0,
    ).astype(f32)


def unit(matrix):
    total = jnp.sum(jnp.sum(matrix * matrix, axis=1, keepdims=True), axis=0, keepdims=True)
    return matrix * (1.0 / jnp.sqrt(total))


def shampoo_kernel(place_ref, own_ref, side_ref, up_ref, cross_ref, left_ref, right_ref, out_ref, pr, plft, xs, zl, got_ref):
    for i, piece in enumerate((own_ref, side_ref, up_ref, cross_ref)):
        got_ref[lax.bitwise_xor(place_ref[0], jnp.int32(i))] = piece[...]
    quarters = []
    for q in range(4):
        quarters.append(unpack_quarter(got_ref[q].astype(f32)))
    h = jnp.concatenate(quarters, axis=0)
    ht = h.T
    xs[...] = h
    zl[...] = eye(BROWS)
    pr[...] = unit(right_ref[...] + dot(left_operand(h), right_operand(ht)))
    plft[...] = unit(left_ref[...] + dot(left_operand(ht), right_operand(h)))

    def sweep(i, carry):
        p = pr[...]
        x = xs[...]
        (ph, pl_), (xh, xl) = halves(p), halves(x)
        p3 = jnp.concatenate([ph, ph, pl_], axis=1)
        high = jnp.concatenate([ph, xh], axis=1)
        both = dot(p3, jnp.concatenate([high, jnp.concatenate([pl_, xl], axis=1), high], axis=0))
        xs[...] = 1.5 * x - 0.5 * both[:, C:]
        q3 = right_operand(0.25 * both[:, :C] - 1.5 * p)
        body = 2.25 * p[:, :256] + dot(p3, q3[:, :256])
        pr[:, :256] = body
        pr[:256, 256:] = body[256:].T
        pr[256:, 256:] = 2.25 * p[256:, 256:] + dot(p3[256:], q3[:, 256:])
        m = plft[...]
        mh, ml = halves(m)
        m3 = jnp.concatenate([mh, ml, mh], axis=0)
        left = jnp.concatenate([mh, mh, ml], axis=1)
        square = dot(left, m3)
        z = zl[...]
        zl[...] = 1.5 * z - 0.5 * dot(left_operand(z), m3)
        plft[...] = 2.25 * m + dot(left, right_operand(0.25 * square - 1.5 * m))
        return carry

    for _ in range(ITERS - 2):
        sweep(0, 0)
    x = xs[...]
    z = zl[...]
    d = (eye(C) - pr[...]).astype(bf16)
    e = (eye(BROWS) - plft[...]).astype(bf16)
    square = dot(e, e)
    z = z + 0.5 * dot(z.astype(bf16), e)
    e = (0.75 * square + 0.25 * dot(e, square.astype(bf16))).astype(bf16)
    z = z + 0.5 * dot(z.astype(bf16), e)
    both = dot(d, jnp.concatenate([d, x.astype(bf16)], axis=1))
    x = x + 0.5 * both[:, C:]
    square = both[:, :C]
    d = (0.75 * square + 0.25 * dot(d, square.astype(bf16))).astype(bf16)
    x = x + 0.5 * dot(d, x.astype(bf16))
    x = dot(left_operand(x), right_operand(z))
    mean = jnp.sum(jnp.sum(x * x, axis=1, keepdims=True), axis=0, keepdims=True) / (C * BROWS)
    x = x * (1.0 / jnp.sqrt(mean + 1e-06))
    for q, (head, tail) in enumerate(pack_block(x)):
        out_ref[q * QPACK : q * QPACK + QROWS, :] = head.astype(bf16)
        out_ref[q * QPACK + QROWS : (q + 1) * QPACK, :] = tail.astype(bf16)


def shampoo(place, pieces, left, right):
    return pl.pallas_call(
        shampoo_kernel,
        out_shape=jax.ShapeDtypeStruct((4 * QPACK, 128), bf16),
        in_specs=[SMEM] + [VMEM] * 6,
        out_specs=VMEM,
        scratch_shapes=[
            pltpu.VMEM((C, C), f32),
            pltpu.VMEM((BROWS, BROWS), f32),
            pltpu.VMEM((C, BROWS), f32),
            pltpu.VMEM((BROWS, BROWS), f32),
            pltpu.VMEM((4, QPACK, 128), bf16),
        ],
        compiler_params=pltpu.CompilerParams(vmem_limit_bytes=40 * 1024 * 1024),
        name="shampoo",
    )(place, *pieces, left, right)


def placed(source, q, parity):
    blank = jnp.zeros((QROWS, BROWS), bf16)
    pieces = []
    for k in range(BLOCKS // 2):
        block = unpack_quarter(source[LAST_ORDER.index(k), q * QPACK : (q + 1) * QPACK, :])
        pieces += [block, blank] if parity == 0 else [blank, block]
    return jnp.concatenate(pieces, axis=1)


def place_kernel(core_ref, mine_ref, out_ref):
    for parity in range(2):

        @pl.when(core_ref[0] == parity)
        def _(parity=parity):
            for q in range(4):
                out_ref[q * QROWS : (q + 1) * QROWS, :] = placed(mine_ref, q, parity)


def join_kernel(core_ref, part_ref, theirs_ref, out_hbm, full, sems):
    def copy(q):
        rows = pl.ds(q * QROWS, QROWS)
        return pltpu.make_async_copy(full.at[rows], out_hbm.at[rows], sems.at[q])

    for parity in range(2):

        @pl.when(core_ref[0] == parity)
        def _(parity=parity):
            for q in range(4):
                rows = slice(q * QROWS, (q + 1) * QROWS)
                full[rows, :] = part_ref[rows, :] + placed(theirs_ref, q, 1 - parity)
                copy(q).start()

    for q in range(4):
        copy(q).wait()


def place(core, mine):
    return pl.pallas_call(
        place_kernel,
        out_shape=jax.ShapeDtypeStruct((C, ROWS), bf16),
        in_specs=[SMEM, VMEM],
        out_specs=VMEM,
        compiler_params=pltpu.CompilerParams(vmem_limit_bytes=20 * 1024 * 1024),
        cost_estimate=pl.CostEstimate(flops=4000000, bytes_accessed=4000000, transcendentals=0),
        name="place",
    )(core, mine)


def join(core, part, theirs):
    return pl.pallas_call(
        join_kernel,
        out_shape=jax.ShapeDtypeStruct((C, ROWS), bf16),
        in_specs=[SMEM, VMEM, VMEM],
        out_specs=HBM,
        scratch_shapes=[pltpu.VMEM((C, ROWS), bf16), pltpu.SemaphoreType.DMA((4,))],
        compiler_params=pltpu.CompilerParams(vmem_limit_bytes=20 * 1024 * 1024),
        name="join",
    )(core, part, theirs)


CORE_SWAP = [(b, b ^ 1) for b in range(16)]
LAST_ORDER = (1, 4, 3, 6, 0, 5, 7, 2)
EIGHTS = [
    [(8 * (k // 4) + 2 * (k % 4) + c) * 16 + 2 * z + ((k // 4) ^ p) for k in LAST_ORDER]
    for c in range(2)
    for z in range(8)
    for p in range(2)
]
WIDE_GROUPS = [
    [(2 * k + c) * 16 + 4 * z + q for q in range(4) for k in range(8)]
    for c in range(2)
    for z in range(4)
]
FAR_GROUPS = [[4 * z + q for z in range(4)] for q in range(4)]
NEAR_GROUPS = [[4 * z + q for q in range(4)] for z in range(4)]


def local(latents, targets, advantages, timesteps, kernel, prior_left, prior_right):
    core = (lax.axis_index("own") % 2).astype(jnp.int32).reshape(1)
    total = float(2 * SPOTS * lax.axis_size("own") * lax.axis_size("rep"))
    mine, theirs = conv_grad(
        total,
        core,
        advantages,
        timesteps,
        latents.reshape(2 * SPOTS, C),
        targets.reshape(2 * SPOTS, C),
        kernel.T,
    )
    theirs = lax.ppermute(theirs, "own", CORE_SWAP)
    pair = (mine + theirs.astype(f32)).astype(bf16)
    pair, left, right = lax.optimization_barrier((pair, BETA * prior_left[0], BETA * prior_right[0]))
    spread = lax.all_to_all(pair, ("own", "rep"), 0, 0, axis_index_groups=WIDE_GROUPS)
    quarter = lax.optimization_barrier(jnp.sum(spread.astype(f32), axis=0)).astype(bf16)
    far = lax.all_to_all(
        jnp.broadcast_to(quarter, (4, QPACK, 128)), "rep", 0, 0, axis_index_groups=FAR_GROUPS
    )
    quarter = lax.optimization_barrier(jnp.sum(far.astype(f32), axis=0)).astype(bf16)
    pieces = [quarter] + [
        lax.ppermute(quarter, "rep", [(r, r ^ i) for r in range(16)]) for i in range(1, 4)
    ]
    spot = (lax.axis_index("rep") % 4).astype(jnp.int32).reshape(1)
    step = shampoo(spot, pieces, left, right)
    mine = lax.all_to_all(
        jnp.broadcast_to(step, (8, 4 * QPACK, 128)), ("own", "rep"), 0, 0, axis_index_groups=EIGHTS
    )
    theirs = lax.ppermute(mine, "own", CORE_SWAP)
    return join(core, place(core, mine), theirs).T


def solution(mesh):
    placed = (
        P(("own", "rep"), None, None, None),
        P(("own", "rep"), None, None, None),
        P(("own", "rep")),
        P(("own", "rep")),
        P(),
        P("own", None, None),
        P("own", None, None),
    )
    return jax.shard_map(local, mesh=mesh, in_specs=placed, out_specs=P(), check_vma=False)
```
